32 devices in a mesh: group: 4 (over x, core), tensor: 4 (over z), dp: 2 (over y).
Axes of the slice: x: 2, y: 2, z: 4, core: 2. Of those that a mesh axis runs over, the one named last changes fastest.
Arguments:
- doc_emb: bfloat16 [48, 4096], P('group', 'dp'), may hold values from -6 to 6
- row_emb: bfloat16 [64, 4096], P(None, 'dp'), may hold values from -6 to 6
- hyper_in: bfloat16 [4096, 8192], P('dp', 'tensor'), may hold values from -0.09375 to 0.09375
- hyper_out: bfloat16 [8192, 8192], P('tensor', 'dp'), may hold values from -0.0625 to 0.0625
- assign: int32 [48], replicated, may hold values from 0 to 47, each once
- states: bfloat16 [2304, 8192], P('group', 'tensor'), may hold values from -6 to 6
- proj_weight: bfloat16 [8192, 8192], P('tensor', 'dp'), may hold values from -0.0625 to 0.0625
- targets: bfloat16 [2304, 8192], P(('group', 'tensor'), 'dp'), may hold values from -6 to 6
Outputs:
- adapted: bfloat16 [2304, 8192], P(('group', 'tensor'), 'dp')
- grad_down: float32 [48, 32, 8192], P('group', None, 'tensor')
- grad_up: float32 [48, 32, 8192], P('group', None, ('dp', 'tensor'))
The draws below stay inside these ranges and needn't reach their ends.
Inputs may be any that keep to these rules, and one draw needn't show every extreme that they name: `assign`: every document is named by exactly one slot.
All inputs are finite; a program needn't handle non-finite values.
Results may differ from the reference program's by a relative error of at most 0.02.
Values may be sent and summed in bfloat16 or wider, within the bound.
No kernel may reach another device: no remote copies, remote signals or barrier semaphores. Data moves between devices by JAX's collectives and lax.ppermute only.
A program may use at most 128 MiB of HBM per device.

```python
import math
import jax
import jax.numpy as jnp
from jax import lax

D = 8192
E = 4096
H = 8192
R = 32
TOK_DOC = 48
DOCS = 48
TOKENS = 2304
N_TENSOR = 4


def block_scale(stream_key, dims, cuts, smallest, high):
    def one(position, shards_of):
        draws = jax.random.uniform(jax.random.fold_in(jax.random.fold_in(stream_key, 6), position), (shards_of,), jnp.float32, smallest / len(cuts), high / len(cuts))
        return jnp.repeat(jnp.exp(draws), dims[position] // shards_of).reshape((-1,) + (1,) * (len(dims) - position - 1))

    factor_of = one(*cuts[0])
    for cut in cuts[1:]:
        factor_of = factor_of * one(*cut)
    return factor_of


def bell_draw(rng, dims, scale, limit, pieces=(), dtype=jnp.bfloat16):
    values = scale * jax.random.normal(rng, dims, jnp.float32)
    if pieces:
        values = values * block_scale(rng, dims, pieces, -0.22, 0.18)
    return jnp.clip(values, -limit, limit).astype(dtype)


def setup_inputs(seed: int = 0) -> dict:
    streams_of = jax.random.split(jax.random.key(seed), 9)
    doc_emb = bell_draw(streams_of[0], (DOCS, E), 1.0, 6.0, ((0, 4), (1, 2)))
    row_emb = bell_draw(streams_of[1], (2 * R, E), 1.0, 6.0, ((1, 2),))
    hyper_in = bell_draw(streams_of[2], (E, H), E ** -0.5, 0.09375, ((0, 2), (1, 4)))
    hyper_out = bell_draw(streams_of[3], (H, D), H ** -0.5, 0.0625, ((0, 4), (1, 2)))
    assign = jax.random.permutation(streams_of[4], DOCS).astype(jnp.int32)
    states = bell_draw(streams_of[5], (TOKENS, D), 1.0, 6.0, ((0, 4), (1, 4)))
    proj_weight = bell_draw(streams_of[6], (D, D), D ** -0.5, 0.0625, ((0, 4), (1, 2)))
    targets = bell_draw(streams_of[7], (TOKENS, D), 1.0, 6.0, ((0, 16), (1, 2)))
    return dict(doc_emb=doc_emb, row_emb=row_emb, hyper_in=hyper_in, hyper_out=hyper_out, assign=assign, states=states, proj_weight=proj_weight, targets=targets)


LOWDIM_MULTIPLE = 0.1

def reference(doc_emb, row_emb, hyper_in, hyper_out, assign, states, proj_weight, targets):
    pre_doc = jnp.dot(doc_emb, hyper_in, preferred_element_type=jnp.float32)
    pre_row = jnp.dot(row_emb, hyper_in, preferred_element_type=jnp.float32)
    hidden = jax.nn.silu(pre_doc[:, None, :] + pre_row[None, :, :]).astype(jnp.bfloat16)
    hidden = hidden.reshape(DOCS * 2 * R, H)
    block_width = H // N_TENSOR
    summed = jnp.zeros((DOCS * 2 * R, D), jnp.float32)
    for block_index in range(N_TENSOR):
        lower = block_index * block_width
        piece = jnp.dot(hidden[:, lower:lower + block_width], hyper_out[lower:lower + block_width, :], preferred_element_type=jnp.float32)
        rounded = lax.optimization_barrier(piece.astype(jnp.bfloat16))
        summed = summed + rounded.astype(jnp.float32)
    factors = summed.astype(jnp.bfloat16).reshape(DOCS, 2 * R, D)
    slot_down = factors[assign, :R, :].astype(jnp.float32)
    slot_up_factor = factors[assign, R:, :].astype(jnp.float32)
    fan_width_multiplier = 1.0 / math.sqrt(D)
    frozen_output = jnp.dot(states, proj_weight, preferred_element_type=jnp.float32)
    bundled_entries = states.astype(jnp.float32).reshape(DOCS, TOK_DOC, D)
    narrow_basis_map = (fan_width_multiplier * jnp.einsum('quw,qlw->qul', bundled_entries, slot_down)).astype(jnp.bfloat16)
    adapter_update = jnp.einsum('ntr,nrc->ntc', narrow_basis_map.astype(jnp.float32), slot_up_factor).reshape(TOKENS, D)
    raised_rows = frozen_output + LOWDIM_MULTIPLE * adapter_update
    adapted = raised_rows.astype(jnp.bfloat16)
    residual = (raised_rows - targets.astype(jnp.float32)).astype(jnp.bfloat16)
    remaining_passages = residual.astype(jnp.float32).reshape(DOCS, TOK_DOC, D)
    position_sensitivity = (LOWDIM_MULTIPLE * jnp.einsum('quw,qlw->qul', remaining_passages, slot_up_factor)).astype(jnp.bfloat16)
    lifting_matrix_sensitivity = LOWDIM_MULTIPLE * jnp.einsum('oed,oec->odc', narrow_basis_map.astype(jnp.float32), remaining_passages)
    lowering_matrix_sensitivity = fan_width_multiplier * jnp.einsum('oed,oec->odc', position_sensitivity.astype(jnp.float32), bundled_entries)
    grad_down = jnp.zeros((DOCS, R, D), jnp.float32).at[assign].set(lowering_matrix_sensitivity)
    grad_up = jnp.zeros((DOCS, R, D), jnp.float32).at[assign].set(lifting_matrix_sensitivity)
    return (adapted, grad_down, grad_up)
```

```python
import math

import jax
import jax.numpy as jnp
from jax import lax
from jax.sharding import PartitionSpec as P

D = 8192
R = 32


LOWDIM_MULTIPLE = 0.1


def spread(block, axis, owner):
    block = jnp.where(lax.axis_index(axis) == owner, block, jnp.zeros_like(block))
    return lax.psum(block, axis)


def hypernet(doc_rows, row_emb, hyper_in, hyper_out):
    doc_count = doc_rows.shape[0]
    pre_doc, pre_row = (
        lax.psum(
            jnp.dot(doc_rows, hyper_in, preferred_element_type=jnp.float32).astype(jnp.bfloat16),
            "dp",
        ).astype(jnp.float32),
        lax.psum(
            jnp.dot(row_emb, hyper_in, preferred_element_type=jnp.float32).astype(jnp.bfloat16),
            "dp",
        ).astype(jnp.float32),
    )
    hidden = jax.nn.silu(pre_doc[:, None, :] + pre_row[None, :, :]).astype(jnp.bfloat16)
    hidden = hidden.reshape(doc_count * 2 * R, hidden.shape[2])
    partial_value = jnp.dot(hidden, hyper_out, preferred_element_type=jnp.float32)
    summed = lax.psum(partial_value.astype(jnp.bfloat16), "tensor")
    factors = summed.reshape(doc_count, 2 * R, hyper_out.shape[1])
    ratio_axes = lax.axis_size("tensor") // lax.axis_size("dp")
    owner_rows = spread(factors[:, :R, :], "dp", lax.axis_index("tensor") // ratio_axes)
    col_width = hyper_out.shape[1] // ratio_axes
    down_block = lax.dynamic_slice_in_dim(
        owner_rows, lax.axis_index("tensor") % ratio_axes * col_width, col_width, 2
    )
    return (down_block, factors[:, R:, :])


def body(doc_emb, row_emb, hyper_in, hyper_out, assign, states, proj_weight, targets):
    doc_count = doc_emb.shape[0]
    group_start = lax.axis_index("group") * doc_count
    slot_docs = lax.dynamic_slice_in_dim(assign, group_start, doc_count)
    everyone = lax.all_gather(doc_emb, "group", axis=0, tiled=True)
    picker = (slot_docs[:, None] == jnp.arange(everyone.shape[0], dtype=jnp.int32)[None, :]).astype(
        jnp.bfloat16
    )
    chosen = jnp.dot(picker, everyone, preferred_element_type=jnp.float32).astype(jnp.bfloat16)
    slot_down, slot_up_factor = hypernet(chosen, row_emb, hyper_in, hyper_out)
    token_count = states.shape[0]
    per_doc = token_count // doc_count
    fan_width_multiplier = 1.0 / math.sqrt(D)
    bundled_entries = states.reshape(doc_count, per_doc, states.shape[1])
    low_part = jnp.einsum(
        "quw,qlw->qul", bundled_entries, slot_down, preferred_element_type=jnp.float32
    ).reshape(token_count, R)
    base_part = jnp.dot(states, proj_weight, preferred_element_type=jnp.float32)
    frozen_output, low_sum = (
        lax.psum_scatter(
            base_part.astype(jnp.bfloat16), "tensor", scatter_dimension=0, tiled=True
        ).astype(jnp.float32),
        lax.psum_scatter(
            low_part.astype(jnp.bfloat16), "tensor", scatter_dimension=0, tiled=True
        ).astype(jnp.float32),
    )
    row_count = frozen_output.shape[0]
    row_start = lax.axis_index("tensor") * row_count
    owner_doc = (row_start + jnp.arange(row_count, dtype=jnp.int32)) // per_doc
    document_member = owner_doc[:, None] == jnp.arange(doc_count, dtype=jnp.int32)[None, :]
    narrow_basis_map = (low_sum * fan_width_multiplier).astype(jnp.bfloat16)
    broadcast_rows = jnp.where(
        document_member[:, :, None], narrow_basis_map[:, None, :], jnp.zeros((), jnp.bfloat16)
    ).reshape(row_count, doc_count * R)
    up_factor_rows = slot_up_factor.reshape(doc_count * R, slot_up_factor.shape[2])
    raised_rows = frozen_output + LOWDIM_MULTIPLE * jnp.dot(
        broadcast_rows, up_factor_rows, preferred_element_type=jnp.float32
    )
    adapted = raised_rows.astype(jnp.bfloat16)
    residual = (raised_rows - targets.astype(jnp.float32)).astype(jnp.bfloat16)
    partial_up_gradient = LOWDIM_MULTIPLE * lax.dot_general(
        broadcast_rows, residual, (((0,), (0,)), ((), ())), preferred_element_type=jnp.float32
    )
    grad_up_local = lax.psum_scatter(
        partial_up_gradient.reshape(doc_count, R, up_factor_rows.shape[1]).astype(jnp.bfloat16),
        "tensor",
        scatter_dimension=2,
        tiled=True,
    ).astype(jnp.float32)
    document_list = lax.dot_general(
        residual, up_factor_rows, (((1,), (1,)), ((), ())), preferred_element_type=jnp.float32
    ).reshape(row_count, doc_count, R)
    token_portion = LOWDIM_MULTIPLE * jnp.sum(
        jnp.where(document_member[:, :, None], document_list, 0.0), axis=1
    )
    placed = lax.dynamic_update_slice_in_dim(
        jnp.zeros((token_count, R), jnp.float32), token_portion, row_start, 0
    )
    position_sensitivity = lax.psum(placed, ("tensor", "dp")).astype(jnp.bfloat16)
    lowering_matrix_sensitivity = fan_width_multiplier * jnp.einsum(
        "oed,oec->odc",
        position_sensitivity.reshape(doc_count, per_doc, R),
        bundled_entries,
        preferred_element_type=jnp.float32,
    )
    own_docs = group_start + jnp.arange(doc_count, dtype=jnp.int32)
    initial_grads = (
        jnp.zeros(
            (
                doc_count,
                lowering_matrix_sensitivity.shape[1] * lowering_matrix_sensitivity.shape[2],
            ),
            jnp.float32,
        ),
        jnp.zeros((doc_count, grad_up_local.shape[1] * grad_up_local.shape[2]), jnp.float32),
    )
    pieces = (
        lax.all_gather(
            lowering_matrix_sensitivity.astype(jnp.bfloat16), "group", axis=0, tiled=True
        ).astype(jnp.float32),
        lax.all_gather(grad_up_local.astype(jnp.bfloat16), "group", axis=0, tiled=True).astype(
            jnp.float32
        ),
    )
    piece_rows = pieces[0].shape[0]
    picker = (own_docs[:, None] == assign[None, :]).astype(jnp.float32)
    first = initial_grads[0] + jnp.dot(
        picker, pieces[0].reshape(piece_rows, -1), precision=lax.Precision.HIGHEST
    )
    second = initial_grads[1] + jnp.dot(
        picker, pieces[1].reshape(piece_rows, -1), precision=lax.Precision.HIGHEST
    )
    grad_down = first.reshape(lowering_matrix_sensitivity.shape)
    grad_up = second.reshape(grad_up_local.shape)
    return (adapted, grad_down, grad_up)


def rotate(n, k):
    return [(i, (i + k) % n) for i in range(n)]


def flip(n, bit):
    return [(i, i ^ bit) for i in range(n)]


def pick(block, index, size=1):
    return lax.dynamic_slice_in_dim(block, index, size, 0)


def gather_flips(block, axis, size):
    blocks = [block]
    bits = []
    bit = size // 2
    order = [0]
    stacked = block[None]
    while bit:
        stacked = jnp.concatenate([stacked, lax.ppermute(stacked, axis, flip(size, bit))], axis=0)
        order = order + [k ^ bit for k in order]
        bit //= 2
    return stacked, order


def line_sum(blocks, place):
    lower = place < 2
    sent = pick(blocks, jnp.where(place == 0, 1, 0), 3)
    outer = lax.ppermute(sent, "tensor", [(0, 1), (3, 2)])
    far = pick(blocks, jnp.where(lower, 2, 0), 2).astype(jnp.float32) + pick(
        outer, jnp.where(lower, 1, 0), 2
    ).astype(jnp.float32)
    middle = lax.ppermute(far.astype(jnp.bfloat16), "tensor", [(1, 2), (2, 1)])
    end = pick(blocks, jnp.where(lower, 0, 3)).astype(jnp.float32) + pick(
        middle, jnp.where(lower, 0, 1)
    ).astype(jnp.float32)
    last = lax.ppermute(end.astype(jnp.bfloat16), "tensor", [(1, 0), (2, 3)])
    return (
        pick(blocks, place).astype(jnp.float32)
        + pick(outer, jnp.where(lower, 0, 2)).astype(jnp.float32)
        + pick(middle, jnp.where(lower, 1, 0)).astype(jnp.float32)
        + last.astype(jnp.float32)
    )[0]


def line_gather(block, place):
    right = [(0, 1), (1, 2), (2, 3)]
    left = [(3, 2), (2, 1), (1, 0)]
    r1 = lax.ppermute(block, "tensor", right)
    l1 = lax.ppermute(block, "tensor", left)
    r2 = lax.ppermute(r1, "tensor", right[1:])
    l2 = lax.ppermute(l1, "tensor", left[1:])
    x3 = lax.ppermute(jnp.where(place == 2, r2, l2), "tensor", [(2, 3), (1, 0)])
    return jnp.stack(
        [block, jnp.where(place == 0, x3, r1), jnp.where(place < 2, l2, r2), jnp.where(place == 3, x3, l1)]
    )


def aligned_body(doc_emb, row_emb, hyper_in, hyper_out, assign, states, proj_weight, targets):
    groups = lax.axis_size("group")
    line = lax.axis_size("tensor")
    group, place, half = (lax.axis_index(a) for a in ("group", "tensor", "dp"))
    docs = doc_emb.shape[0]
    mine = docs // line
    per_doc = states.shape[0] // docs
    in_width = states.shape[1]
    out_width = proj_weight.shape[1]
    hidden_width = hyper_in.shape[1]
    scale = 1.0 / math.sqrt(in_width * line)
    f32, bf16 = jnp.float32, jnp.bfloat16

    slot_docs = lax.dynamic_slice_in_dim(assign, group * docs, docs)
    embs, order = gather_flips(doc_emb, "group", groups)
    flips = jnp.array(order, jnp.int32)
    there = (group ^ flips)[:, None] * docs + jnp.arange(docs, dtype=jnp.int32)[None, :]
    chooser = (slot_docs[:, None] == there.reshape(1, -1)).astype(bf16)
    chosen = jnp.dot(
        chooser, embs.reshape(groups * docs, -1), preferred_element_type=f32
    ).astype(bf16)

    by_slot = states.reshape(line, mine, per_doc, in_width)
    targets = targets.reshape(mine, per_doc, out_width)
    base = []
    for k in range(mine):
        part = jnp.dot(
            by_slot[:, k].reshape(line * per_doc, in_width), proj_weight, preferred_element_type=f32
        ).astype(bf16)
        base.append(line_sum(part.reshape(line, per_doc, out_width), place))

    moved, _ = gather_flips(states, "group", groups)
    own_docs = group * docs + jnp.arange(docs, dtype=jnp.int32)
    owner = (own_docs[:, None] == assign[there.reshape(-1)][None, :]).astype(bf16)
    own_states = jnp.dot(
        owner, moved.reshape(groups * docs, per_doc * in_width), preferred_element_type=f32
    ).astype(bf16).reshape(docs, per_doc, in_width)

    pre = jnp.dot(
        jnp.concatenate([row_emb, chosen], axis=0), hyper_in, preferred_element_type=f32
    ).astype(bf16)
    pre = pre.astype(f32) + lax.ppermute(pre, "dp", rotate(2, 1)).astype(f32)
    pre_row, pre_doc = pre[: 2 * R], pre[2 * R :]

    def hidden_of(doc_part, row_part):
        return jax.nn.silu(doc_part[:, None, :] + row_part[None, :, :]).astype(bf16)

    tokens_half = states.shape[0] // 2
    piece = lax.dynamic_slice_in_dim(states, half * tokens_half, tokens_half, 0)
    line_states = line_gather(piece, place)

    def columns_of(which):
        return jnp.concatenate(
            [pick(line_states, (place - 2 * which - b) % line)[0] for b in range(2)], axis=1
        )

    kept = columns_of(half)
    given = lax.ppermute(columns_of(1 - half), "dp", rotate(2, 1))
    wide = jnp.concatenate([kept, given], axis=0)
    through = lax.dot_general(
        wide, hyper_out, (((1,), (1,)), ((), ())), preferred_element_type=f32
    ).astype(bf16)
    turned = jnp.where(half == 0, pre_doc, jnp.roll(pre_doc, docs // 2, axis=0))
    hidden_down = hidden_of(turned, pre_row[:R])
    low = jnp.einsum(
        "quw,qlw->qul",
        through.reshape(docs, per_doc, hidden_width),
        hidden_down,
        preferred_element_type=f32,
    ).reshape(states.shape[0], R)
    low = low + lax.ppermute(jnp.roll(low, tokens_half, axis=0), "dp", rotate(2, 1))
    low = low.reshape(line, mine * per_doc, R)
    low_mine = pick(low, (place - 2 * half) % line)
    for k in range(1, line):
        low_mine = low_mine + lax.ppermute(
            pick(low, (place + k - 2 * half) % line), "tensor", rotate(line, k)
        )
    narrow = (low_mine[0] * scale).astype(bf16).reshape(mine, per_doc, R)

    hidden_up = hidden_of(pre_doc, pre_row[R:]).reshape(line, mine, R, hidden_width)
    adapted, up_out = [], []
    quarter = out_width // line
    for k in range(mine):
        part = jnp.dot(
            hidden_up[:, k].reshape(line * R, hidden_width), hyper_out, preferred_element_type=f32
        ).astype(bf16)
        up = line_sum(part.reshape(line, R, out_width), place).astype(bf16)
        raised = base[k] + LOWDIM_MULTIPLE * jnp.dot(narrow[k], up, preferred_element_type=f32)
        adapted.append(raised.astype(bf16))
        residual = (raised - targets[k].astype(f32)).astype(bf16)
        token = LOWDIM_MULTIPLE * lax.dot_general(
            up, residual, (((1,), (1,)), ((), ())), preferred_element_type=f32
        )
        token = (token + lax.ppermute(token, "dp", rotate(2, 1))).astype(bf16)
        token = jnp.pad(token, ((0, 0), (0, 128 - per_doc)))
        up_grad = (
            LOWDIM_MULTIPLE
            * lax.dot_general(
                narrow[k], residual, (((0,), (0,)), ((), ())), preferred_element_type=f32
            )
        ).astype(bf16)
        got = []
        for r in range(line):
            block = jnp.concatenate(
                [
                    lax.dynamic_slice_in_dim(up_grad, (place + r) % line * quarter, quarter, 1),
                    token,
                ],
                axis=1,
            )
            got.append(lax.ppermute(block, "tensor", rotate(line, r)) if r else block)
        everyone, _ = gather_flips(jnp.stack(got), "group", groups)
        up_out.append(everyone)

    places = (place - jnp.arange(line, dtype=jnp.int32)) % line
    slots = (
        (group ^ flips)[None, :, None] * docs
        + places[None, None, :] * mine
        + jnp.arange(mine, dtype=jnp.int32)[:, None, None]
    ).reshape(-1)
    taker = (own_docs[:, None] == assign[slots][None, :]).astype(bf16)
    gathered = jnp.stack(up_out).reshape(mine * groups * line, R, quarter + 128)
    grad_up = jnp.dot(
        taker,
        gathered[:, :, :quarter].reshape(-1, R * quarter),
        preferred_element_type=f32,
    ).reshape(docs, R, quarter)
    tokens = jnp.dot(
        taker, gathered[:, :, quarter:].reshape(-1, R * 128), preferred_element_type=f32
    ).astype(bf16).reshape(docs, R, 128)[:, :, :per_doc]
    grad_down = scale * jnp.einsum(
        "ode,oec->odc", tokens, own_states, preferred_element_type=f32
    )
    return (jnp.concatenate(adapted, axis=0), grad_down, grad_up)


def solution(mesh):
    in_specs = (
        P("group", "dp"),
        P(None, "dp"),
        P("dp", "tensor"),
        P("tensor", "dp"),
        P(),
        P("group", "tensor"),
        P("tensor", "dp"),
        P(("group", "tensor"), "dp"),
    )
    out_specs = (
        P(("group", "tensor"), "dp"),
        P("group", None, "tensor"),
        P("group", None, ("dp", "tensor")),
    )
    groups, line, halves = (mesh.shape[a] for a in ("group", "tensor", "dp"))

    def step(*arrays):
        docs = arrays[0].shape[0] // groups
        fits = line == 4 and halves == 2 and groups & (groups - 1) == 0 and docs % line == 0
        plan = aligned_body if fits and docs % 2 == 0 else body
        return jax.shard_map(plan, mesh=mesh, in_specs=in_specs, out_specs=out_specs, check_vma=False)(*arrays)

    return step
```
